128 devices in a mesh: ctx: 16 (over x, y_hi, core), head: 8 (over y_lo, z).
Axes of the slice: x: 4, y: 4 (y_hi: 2, y_lo: 2; y = y_hi * 2 + y_lo), z: 4, core: 2. Of those that a mesh axis runs over, the one named last changes fastest.
Arguments:
- queries: bfloat16 [6144, 8192], P('ctx', 'head')
- query_scale: bfloat16 [6144, 64], P('ctx', 'head'), may hold values from 0.25 to 4
- keys: bfloat16 [6144, 1024], P('ctx', 'head')
- key_scale: bfloat16 [6144, 8], P('ctx', 'head'), may hold values from 0.4 to 2
- values: bfloat16 [6144, 1024], P('ctx', 'head'), may hold values from -6 to 6
- value_scale: bfloat16 [6144, 8], P('ctx', 'head'), may hold values from 0.5 to 2
- block_mask: int32 [48, 48], replicated, may hold values from 0 to 1, as said below
- out_weight: bfloat16 [8192, 8192], P('head'), may hold values from -0.5 to 0.5
- out_scale: float32 [8192], P('head'), may hold values from 0.5 to 2
Outputs:
- output: bfloat16 [6144, 8192], P('ctx', 'head')
The draws below stay inside these ranges and needn't reach their ends.
Inputs may be any that keep to these rules, and one draw needn't show every extreme that they name: block_mask[i, j] is 0 for j > i and 1 for j = i.
All inputs are finite; a program needn't handle non-finite values.
Results may differ from the reference program's by a relative error of at most 0.02.
Values may be sent and summed in bfloat16 or wider, within the bound.
No kernel may reach another device: no remote copies, remote signals or barrier semaphores. Data moves between devices by JAX's collectives and lax.ppermute only.
A program may use at most 128 MiB of HBM per device.

```python
import math
import jax
import jax.numpy as jnp
from jax import lax

D = 8192
HD = 128
KEY_VALUE_HEADS = 8
GROUP = 8
BLK = 128
QH = 64
SEQUENCE_LENGTH = 6144
NBLK = 48
N_HEAD = 8


def joint_draw(key):
    key_q = jax.random.fold_in(key, 101)
    key_k = jax.random.fold_in(key, 202)
    key_qs = jax.random.fold_in(key, 303)
    key_column_blocks = jax.random.fold_in(key, 404)
    queries = jax.random.truncated_normal(key_q, -6.0, 6.0, (SEQUENCE_LENGTH, QH * HD), jnp.float32)
    keys = jax.random.truncated_normal(key_k, -6.0, 6.0, (SEQUENCE_LENGTH, KEY_VALUE_HEADS * HD), jnp.float32)
    query_dequant_scale = jnp.exp(jax.random.uniform(key_qs, (SEQUENCE_LENGTH, QH), jnp.float32, jnp.log(0.25), jnp.log(4.0)))
    key_dequant_scale = jnp.exp(jax.random.uniform(key_column_blocks, (SEQUENCE_LENGTH, KEY_VALUE_HEADS), jnp.float32, jnp.log(0.4), jnp.log(2.0)))
    return (queries, query_dequant_scale, keys, key_dequant_scale)


def draw_queries(key, part):
    return joint_draw(key)[0].astype(jnp.bfloat16)


def draw_query_scale(key, part):
    return joint_draw(key)[1].astype(jnp.bfloat16)


def draw_keys(key, part):
    return joint_draw(key)[2].astype(jnp.bfloat16)


def draw_key_scale(key, part):
    return joint_draw(key)[3].astype(jnp.bfloat16)


def draw_block_mask(key, part):
    coins = jax.random.randint(jax.random.fold_in(key, 505), (NBLK, NBLK), 0, 2, jnp.int32)
    rows = jnp.arange(NBLK, dtype=jnp.int32)[:, None]
    cols = jnp.arange(NBLK, dtype=jnp.int32)[None, :]
    table = jnp.where(cols < rows, coins, 0)
    return jnp.where(cols == rows, 1, table).astype(jnp.int32)


def shard_levels(key, extent, pieces, smallest, high):
    def one(axis_at, shards_of):
        steps = jax.random.uniform(jax.random.fold_in(jax.random.fold_in(key, 6), axis_at), (shards_of,), jnp.float32, smallest / len(pieces), high / len(pieces))
        return jnp.repeat(jnp.exp(steps), extent[axis_at] // shards_of).reshape((-1,) + (1,) * (len(extent) - axis_at - 1))

    factor_of = one(*pieces[0])
    for cut in pieces[1:]:
        factor_of = factor_of * one(*cut)
    return factor_of


def bell_draw(stream_key, shape, deviation, reach, shards=(), kind=jnp.bfloat16):
    loudness = shard_levels(stream_key, shape, shards, -0.22, 0.18) if shards else 1.0
    entries = jax.random.normal(stream_key, shape, jnp.float32) * deviation * loudness
    return jnp.minimum(jnp.maximum(entries, -reach), reach).astype(kind)


def setup_inputs(seed: int = 0) -> dict:
    arg_keys = jax.random.split(jax.random.key(seed), 10)
    queries = draw_queries(jax.random.fold_in(arg_keys[9], 71), 0)
    query_scale = draw_query_scale(jax.random.fold_in(arg_keys[9], 71), 0)
    keys = draw_keys(jax.random.fold_in(arg_keys[9], 71), 0)
    key_scale = draw_key_scale(jax.random.fold_in(arg_keys[9], 71), 0)
    values = bell_draw(arg_keys[4], (SEQUENCE_LENGTH, KEY_VALUE_HEADS * HD), 1.0, 6.0, ((0, 16), (1, 8)))
    value_scale = jnp.clip(jnp.exp(math.log(2.0) - 1.3862944 * jax.random.uniform(arg_keys[5], (SEQUENCE_LENGTH, KEY_VALUE_HEADS), jnp.float32) ** shard_levels(arg_keys[5], (SEQUENCE_LENGTH, KEY_VALUE_HEADS), ((0, 16), (1, 8)), -0.2, 0.2)), 0.5, 2.0).astype(jnp.bfloat16)
    block_mask = draw_block_mask(jax.random.fold_in(arg_keys[9], 71), 0)
    out_weight = bell_draw(arg_keys[7], (QH * HD, D), HD ** -0.5, 0.5, ((0, 8),))
    out_scale = jnp.clip(jnp.exp(math.log(2.0) - 1.3862944 * jax.random.uniform(arg_keys[8], (D,), jnp.float32) ** shard_levels(arg_keys[8], (D,), ((0, 8),), -0.2, 0.2)), 0.5, 2.0)
    return dict(queries=queries, query_scale=query_scale, keys=keys, key_scale=key_scale, values=values, value_scale=value_scale, block_mask=block_mask, out_weight=out_weight, out_scale=out_scale)


NEG_FILL = -1e+30

def reference(queries, query_scale, keys, key_scale, values, value_scale, block_mask, out_weight, out_scale):
    total_rows = queries.shape[0]
    heads_q = queries.shape[1] // HD
    kv_heads = keys.shape[1] // HD
    keys3 = keys.reshape(total_rows, kv_heads, HD).astype(jnp.float32)
    vals3 = values.reshape(total_rows, kv_heads, HD).astype(jnp.float32)
    key_sc = key_scale.astype(jnp.float32)
    val_sc = value_scale.astype(jnp.float32)
    key_pos = jnp.arange(total_rows, dtype=jnp.int32)
    key_block = key_pos // BLK
    inv_root = 1.0 / jnp.sqrt(jnp.float32(HD))

    def one_block(index):
        first = (index * BLK).astype(jnp.int32)
        q_rows = lax.dynamic_slice_in_dim(queries, first, BLK, 0).reshape(BLK, kv_heads, GROUP, HD).astype(jnp.float32)
        q_sc = lax.dynamic_slice_in_dim(query_scale, first, BLK, 0).astype(jnp.float32).reshape(BLK, kv_heads, GROUP)
        raw = jnp.einsum('rkgd,nkd->kgrn', q_rows, keys3, precision=lax.Precision.HIGHEST)
        scores = raw * jnp.transpose(q_sc, (1, 2, 0))[..., None] * key_sc.T[:, None, None, :] * inv_root
        q_pos = first + jnp.arange(BLK, dtype=jnp.int32)
        mask_row = lax.dynamic_index_in_dim(block_mask, index, 0, keepdims=False)
        block_ok = mask_row[key_block] == 1
        allowed = block_ok[None, :] & (key_pos[None, :] <= q_pos[:, None])
        scores = jnp.where(allowed[None, None], scores, NEG_FILL)
        top = lax.optimization_barrier(jnp.max(scores, axis=3))
        expo = jnp.where(allowed[None, None], jnp.exp(scores - top[..., None]), 0.0)
        total = lax.optimization_barrier(jnp.sum(expo, axis=3))
        weights = lax.optimization_barrier((expo * val_sc.T[:, None, None, :]).astype(jnp.bfloat16)).astype(jnp.float32)
        mixed = jnp.einsum('kgrn,nkd->kgrd', weights, vals3, precision=lax.Precision.HIGHEST)
        attended = mixed / total[..., None]
        return jnp.transpose(attended, (2, 0, 1, 3)).reshape(BLK, heads_q * HD).astype(jnp.bfloat16)
    blocks = lax.map(one_block, jnp.arange(total_rows // BLK, dtype=jnp.int32))
    attended = blocks.reshape(total_rows, heads_q * HD)
    rows_group = heads_q * HD // N_HEAD

    def add_group(group, summed):
        offset = (group * rows_group).astype(jnp.int32)
        cols = lax.dynamic_slice_in_dim(attended, offset, rows_group, 1)
        rows = lax.dynamic_slice_in_dim(out_weight, offset, rows_group, 0)
        part = jnp.dot(cols, rows, preferred_element_type=jnp.float32)
        part = lax.optimization_barrier(part.astype(jnp.bfloat16)).astype(jnp.float32)
        return summed + part
    summed = lax.fori_loop(0, N_HEAD, add_group, jnp.zeros((total_rows, out_weight.shape[1]), jnp.float32))
    return (summed * out_scale[None, :]).astype(jnp.bfloat16)
```

```python
import functools
import math

import jax
import jax.numpy as jnp
from jax import lax
from jax.experimental import pallas as pl
from jax.experimental.pallas import tpu as pltpu
from jax.sharding import PartitionSpec as P

HD = 128
GROUP = 8
BLK = 128
RANK_BLOCKS = 3
CHIPS = 8
QSCALE = math.log2(math.e) / math.sqrt(HD)
F32 = jnp.float32
BF16 = jnp.bfloat16


def fold_blocks(blocks, causal, kv, qt, top, total, accum):
    keys = jnp.concatenate([kv[b, :, :HD] for b in blocks], axis=0)
    vals_t = jnp.concatenate([kv[b, :, HD:] for b in blocks], axis=1)
    for pair in range(GROUP // 2):
        cols = pl.ds(pair * 2 * BLK, 2 * BLK)
        scores = jnp.dot(keys, qt[:, cols], preferred_element_type=F32)
        if causal:
            key_at = lax.broadcasted_iota(jnp.int32, scores.shape, 0)
            row_at = lax.broadcasted_iota(jnp.int32, scores.shape, 1) % BLK
            scores = jnp.where(key_at <= row_at, scores, -jnp.inf)
            new_top = jnp.max(scores, axis=0, keepdims=True)
            expo = jnp.exp2(scores - new_top)
            total[:, cols] = jnp.sum(expo, axis=0, keepdims=True)
            accum[:, cols] = jnp.dot(vals_t, expo.astype(BF16), preferred_element_type=F32)
        else:
            old_top = top[:, cols]
            new_top = jnp.maximum(old_top, jnp.max(scores, axis=0, keepdims=True))
            expo = jnp.exp2(scores - new_top)
            decay = jnp.exp2(old_top - new_top)
            total[:, cols] = total[:, cols] * decay + jnp.sum(expo, axis=0, keepdims=True)
            accum[:, cols] = accum[:, cols] * decay + jnp.dot(
                vals_t, expo.astype(BF16), preferred_element_type=F32
            )
        top[:, cols] = new_top


def attend_kernel(
    first_of, place, mask, q_ref, qs_ref, mine, other, o_ref, kv, qt, top, total, accum, todo, sems
):
    chip, core = place[0], place[1]

    def copies():
        made = []
        for which, source in ((0, mine), (1, other)):
            for shift in range(CHIPS):
                owner = 2 * lax.rem(chip - shift + CHIPS, CHIPS) + lax.rem(core + which, 2)
                made.append(
                    pltpu.make_async_copy(
                        source.at[pl.ds(shift * RANK_BLOCKS, RANK_BLOCKS)],
                        kv.at[pl.ds(owner * RANK_BLOCKS, RANK_BLOCKS)],
                        sems.at[which * CHIPS + shift],
                    )
                )
        return made

    @pl.when(pl.program_id(0) == 0)
    def _():
        for copy in copies():
            copy.start()

    row_block = first_of[0] + pl.program_id(0)
    for head in range(GROUP):
        cols = pl.ds(head * HD, HD)
        scale = qs_ref[:, head : head + 1].astype(F32) * QSCALE
        qt[:, cols] = (q_ref[:, cols].astype(F32) * scale).T.astype(BF16)

    def list_block(block, count):
        @pl.when(mask[row_block, block] == 1)
        def _():
            todo[count] = block

        return count + jnp.where(mask[row_block, block] == 1, 1, 0)

    count = lax.fori_loop(0, row_block, list_block, jnp.int32(0))

    @pl.when(pl.program_id(0) == 0)
    def _():
        for copy in copies():
            copy.wait()

    state = (kv, qt, top, total, accum)
    fold_blocks([row_block], True, *state)

    @pl.loop(0, count // 4)
    def _(step):
        fold_blocks([todo[4 * step + i] for i in range(4)], False, *state)

    @pl.when(count % 4 >= 2)
    def _():
        at = count // 4 * 4
        fold_blocks([todo[at], todo[at + 1]], False, *state)

    @pl.when(count % 2 == 1)
    def _():
        fold_blocks([todo[count - 1]], False, *state)

    for head in range(GROUP):
        cols = pl.ds(head * HD, HD)
        o_ref[:, cols] = (accum[:, cols] / total[:, cols]).T.astype(BF16)


def attend(first_block, place, mask, queries, query_scale, mine, other, rows):
    smem = pl.BlockSpec(memory_space=pltpu.SMEM)
    blocks = mask.shape[0]
    count = rows // BLK
    wide = GROUP * HD
    return pl.pallas_call(
        attend_kernel,
        grid=(count,),
        out_shape=jax.ShapeDtypeStruct((rows, wide), BF16),
        in_specs=[
            smem,
            smem,
            smem,
            pl.BlockSpec((BLK, wide), lambda i: (i, 0)),
            pl.BlockSpec((BLK, GROUP), lambda i: (i, 0)),
            pl.BlockSpec(memory_space=pl.ANY),
            pl.BlockSpec(memory_space=pl.ANY),
        ],
        out_specs=pl.BlockSpec((BLK, wide), lambda i: (i, 0)),
        scratch_shapes=[
            pltpu.VMEM((blocks, BLK, 2 * HD), BF16),
            pltpu.VMEM((HD, wide), BF16),
            pltpu.VMEM((1, wide), F32),
            pltpu.VMEM((1, wide), F32),
            pltpu.VMEM((HD, wide), F32),
            pltpu.SMEM((blocks,), jnp.int32),
            pltpu.SemaphoreType.DMA((2 * CHIPS,)),
        ],
        compiler_params=pltpu.CompilerParams(vmem_limit_bytes=32 << 20),
        cost_estimate=pl.CostEstimate(
            flops=4 * rows * wide * blocks * BLK // 2,
            bytes_accessed=blocks * BLK * HD * 4 + rows * wide * 4,
            transcendentals=rows * GROUP * blocks * BLK // 2,
        ),
        name="attend",
    )(first_block, place, mask, queries, query_scale, mine, other)


def pack(keys, key_scale, values, value_scale):
    scaled_k = keys.astype(F32) * key_scale.astype(F32)
    scaled_v = values.astype(F32) * value_scale.astype(F32)
    k3 = scaled_k.astype(BF16).reshape(RANK_BLOCKS, BLK, HD)
    v3 = jnp.transpose(scaled_v.astype(BF16).reshape(RANK_BLOCKS, BLK, HD), (0, 2, 1))
    return jnp.concatenate([k3, v3], axis=2)


def gather(packed):
    got = [packed]
    for shift in range(1, CHIPS):
        pairs = [(2 * a + c, 2 * (a + shift) + c) for a in range(CHIPS - shift) for c in range(2)]
        got.append(lax.ppermute(packed, "ctx", pairs))
    mine = jnp.concatenate(got, axis=0)
    other = lax.ppermute(mine, "ctx", [(i, i ^ 1) for i in range(2 * CHIPS)])
    return mine, other


def local(
    queries, query_scale, keys, key_scale, values, value_scale, block_mask, out_weight, out_scale
):
    rows = queries.shape[0]
    rank = lax.axis_index("ctx").astype(jnp.int32)
    place = jnp.stack([rank // 2, rank % 2])
    mine, other = gather(pack(keys, key_scale, values, value_scale))
    attended = attend(
        (rank * RANK_BLOCKS)[None], place, block_mask, queries, query_scale, mine, other, rows
    )
    projected = jnp.dot(attended, out_weight, preferred_element_type=F32)
    summed = lax.psum_scatter(
        projected.astype(BF16), "head", scatter_dimension=1, tiled=True
    ).astype(F32)
    return (summed * out_scale[None, :]).astype(BF16)


def solution(mesh):
    return jax.shard_map(
        local,
        mesh=mesh,
        in_specs=(
            P("ctx", "head"),
            P("ctx", "head"),
            P("ctx", "head"),
            P("ctx", "head"),
            P("ctx", "head"),
            P("ctx", "head"),
            P(),
            P("head", None),
            P("head"),
        ),
        out_specs=P("ctx", "head"),
        check_vma=False,
    )
```

```python
import math

import jax
import jax.numpy as jnp
from jax import lax
from jax.experimental import pallas as pl
from jax.experimental.pallas import tpu as pltpu
from jax.sharding import PartitionSpec as P

HD = 128
GROUP = 8
BLK = 128
RANK_BLOCKS = 3
CHIPS = 8
DEPTH = 4
HEADS = 8
WIDE = GROUP * HD
QSCALE = math.log2(math.e) / math.sqrt(HD)
F32 = jnp.float32
BF16 = jnp.bfloat16
CHUNKS = ((0, 2), (2, 1))
VMEM = 56 << 20
PARTS = 2


def fold_blocks(count, causal, kv, qt, qrow, top, total, accum):
    keys = jnp.concatenate([kv[b, :, :HD] for b in range(count)], axis=0)
    vals_t = jnp.concatenate([kv[b, :, HD:] for b in range(count)], axis=1)
    span = 2 * BLK
    steps = WIDE // span
    raws = [
        jnp.dot(keys, qt[:, pl.ds(step * span, span)], preferred_element_type=F32)
        for step in range(steps)
    ]
    for step in range(steps):
        cols = pl.ds(step * span, span)
        scores = raws[step] * qrow[:, cols]
        if causal:
            key_at = lax.broadcasted_iota(jnp.int32, (BLK, span), 0)
            row_at = lax.broadcasted_iota(jnp.int32, (BLK, span), 1) % BLK
            own = jnp.where(key_at <= row_at, scores[:BLK], -jnp.inf)
            scores = jnp.concatenate([own, scores[BLK:]], axis=0) if count > 1 else own
            new_top = jnp.max(scores, axis=0, keepdims=True)
            expo = jnp.exp2(scores - new_top)
            total[:, cols] = jnp.sum(expo, axis=0, keepdims=True)
            accum[:, cols] = jnp.dot(vals_t, expo.astype(BF16), preferred_element_type=F32)
        else:
            old_top = top[:, cols]
            new_top = jnp.maximum(old_top, jnp.max(scores, axis=0, keepdims=True))
            expo = jnp.exp2(scores - new_top)
            decay = jnp.exp2(old_top - new_top)
            total[:, cols] = total[:, cols] * decay + jnp.sum(expo, axis=0, keepdims=True)
            accum[:, cols] = accum[:, cols] * decay + jnp.dot(
                vals_t, expo.astype(BF16), preferred_element_type=F32
            )
        top[:, cols] = new_top


def attend_rows(
    first, place, mask, q_ref, qs_ref, mine, other, kv, qt, qrow, top, total, accum, todo, sems
):
    chip, core = place[0], place[1]
    row_block = place[2] + pl.program_id(0)
    column = lax.rem(chip, 2) if first else 1 - lax.rem(chip, 2)
    base = 1 if first else 0

    def fetch(block, slot, at):
        owner = block // RANK_BLOCKS
        index = (chip // 2 - owner // 4) * RANK_BLOCKS + block % RANK_BLOCKS
        for same, source in ((True, mine), (False, other)):

            @pl.when((owner % 2 == core) == same)
            def _():
                pltpu.make_async_copy(source.at[index], kv.at[slot, at], sems.at[slot, at]).start()

    def arrive(slot, at):
        pltpu.make_async_copy(mine.at[0], kv.at[slot, at], sems.at[slot, at]).wait()

    if first:
        fetch(row_block, 0, 0)

    def list_block(block, count):
        todo[count] = block
        wanted = lax.rem(block // (2 * RANK_BLOCKS), 2) == column
        return count + jnp.where(wanted, mask[row_block, block], 0)

    count = lax.fori_loop(0, row_block, list_block, jnp.int32(0))
    rest = count % DEPTH
    full = count // DEPTH
    for at in range(DEPTH - 1):

        @pl.when(at < rest)
        def _():
            fetch(todo[at], 0, at + base)

    def fetch_group(step, slot):
        for at in range(DEPTH):
            fetch(todo[rest + step * DEPTH + at], slot, at)

    @pl.when(full > 0)
    def _():
        fetch_group(0, 1)

    scale = qs_ref[...].astype(F32).T * QSCALE
    for head in range(GROUP):
        cols = pl.ds(head * HD, HD)
        qt[:, cols] = q_ref[:, cols].T
        qrow[:, cols] = scale[head : head + 1]

    state = (qt, qrow, top, total, accum)
    if first:
        arrive(0, 0)
    for extra in range(1 - base, DEPTH):

        @pl.when(rest == extra)
        def _():
            for at in range(extra):
                arrive(0, at + base)
            fold_blocks(extra + base, first, kv.at[0], *state)

    @pl.loop(0, full)
    def _(step):
        slot = (step + 1) % 2

        @pl.when(step + 1 < full)
        def _():
            fetch_group(step + 1, 1 - slot)

        for at in range(DEPTH):
            arrive(slot, at)
        fold_blocks(DEPTH, False, kv.at[slot], *state)


def first_kernel(
    place, mask, q_ref, qs_ref, mine, other, top, total, accum, kv, qt, qrow, todo, sems
):
    rows = (place, mask, q_ref, qs_ref, mine, other, kv, qt, qrow)
    attend_rows(True, *rows, top.at[0], total.at[0], accum.at[0], todo, sems)


def second_kernel(
    place, mask, q_ref, qs_ref, mine, other, top_in, total_in, accum_in, o_ref,
    kv, qt, qrow, top, total, accum, todo, sems,
):
    top[...] = top_in[0]
    total[...] = total_in[0]
    accum[...] = accum_in[0]
    rows = (place, mask, q_ref, qs_ref, mine, other, kv, qt, qrow)
    attend_rows(False, *rows, top, total, accum, todo, sems)
    for head in range(GROUP):
        cols = pl.ds(head * HD, HD)
        o_ref[:, cols] = (accum[:, cols] * (1.0 / total[:, cols])).astype(BF16).T


def attend(place, mask, queries, query_scale, mine, other, chunk, state):
    first, count = chunk
    blocks = mask.shape[0]
    smem = pl.BlockSpec(memory_space=pltpu.SMEM)
    hbm = pl.BlockSpec(memory_space=pl.ANY)
    in_specs = [
        smem,
        smem,
        pl.BlockSpec((BLK, WIDE), lambda i: (first + i, 0)),
        pl.BlockSpec((BLK, GROUP), lambda i: (first + i, 0)),
        hbm,
        hbm,
    ]
    row = pltpu.VMEM((1, WIDE), F32)
    held = [
        pl.BlockSpec((1, 1, WIDE), lambda i: (first + i, 0, 0)),
        pl.BlockSpec((1, 1, WIDE), lambda i: (first + i, 0, 0)),
        pl.BlockSpec((1, HD, WIDE), lambda i: (first + i, 0, 0)),
    ]
    kv = [pltpu.VMEM((2, DEPTH, BLK, 2 * HD), BF16), pltpu.VMEM((HD, WIDE), BF16), row]
    tail = [pltpu.SMEM((blocks,), jnp.int32), pltpu.SemaphoreType.DMA((2, DEPTH))]
    common = dict(
        grid=(count,),
        compiler_params=pltpu.CompilerParams(vmem_limit_bytes=VMEM),
        cost_estimate=pl.CostEstimate(
            flops=count * BLK * WIDE * 4 * 2500,
            bytes_accessed=count * blocks * BLK * HD * 2,
            transcendentals=count * BLK * GROUP * 2500,
        ),
    )
    args = (
        place + jnp.array([0, 0, first], jnp.int32),
        mask,
        queries,
        query_scale,
        mine,
        other,
    )
    if state is None:
        return pl.pallas_call(
            first_kernel,
            in_specs=in_specs,
            out_specs=held,
            out_shape=[
                jax.ShapeDtypeStruct((count, 1, WIDE), F32),
                jax.ShapeDtypeStruct((count, 1, WIDE), F32),
                jax.ShapeDtypeStruct((count, HD, WIDE), F32),
            ],
            scratch_shapes=kv + tail,
            name="attend_first",
            **common,
        )(*args)
    return pl.pallas_call(
        second_kernel,
        in_specs=in_specs + held,
        out_specs=pl.BlockSpec((BLK, WIDE), lambda i: (i, 0)),
        out_shape=jax.ShapeDtypeStruct((count * BLK, WIDE), BF16),
        scratch_shapes=kv + [row, row, pltpu.VMEM((HD, WIDE), F32)] + tail,
        name="attend_second",
        **common,
    )(*args, *state)


def pack(keys, key_scale, values, value_scale):
    scaled_k = keys.astype(F32) * key_scale.astype(F32)
    scaled_v = values.astype(F32) * value_scale.astype(F32)
    k3 = scaled_k.astype(BF16).reshape(RANK_BLOCKS, BLK, HD)
    v3 = jnp.transpose(scaled_v.astype(BF16).reshape(RANK_BLOCKS, BLK, HD), (0, 2, 1))
    return jnp.concatenate([k3, v3], axis=2)


CORE_SWAP = [(i, i ^ 1) for i in range(2 * CHIPS)]


def along_x(block):
    got = [block]
    for shift in range(1, 4):
        pairs = [(4 * x + i, 4 * (x + shift) + i) for x in range(4 - shift) for i in range(4)]
        got.append(lax.ppermute(block, "ctx", pairs))
    return got


def with_core(got):
    mine = jnp.concatenate(got, axis=0)
    return mine, lax.ppermute(mine, "ctx", CORE_SWAP)


def across_y():
    pairs = []
    for x in range(4):
        for y in range(4):
            for core in range(2):
                for z in range(4):
                    far = (y + (1 if core == 0 else 3)) % 4
                    start = ((x * 2 + y // 2) * 2 + core) * HEADS + (y % 2) * 4 + z
                    end = ((x * 2 + far // 2) * 2 + core) * HEADS + (far % 2) * 4 + z
                    pairs.append((start, end))
    return pairs


def cut_weights(weight, core, half):
    rows, width = weight.shape
    keep = rows // 2
    return lax.dynamic_slice(weight, (core * keep, (1 - half) * (width // 2)), (keep, width // 2))


def project_kernel(info, *refs):
    chunks = len(CHUNKS)
    own, near, far = refs[:chunks], refs[chunks : 2 * chunks], refs[2 * chunks : 3 * chunks]
    w_own, w_near, w_far = refs[3 * chunks : 3 * chunks + 3]
    outs = refs[3 * chunks + 3 :]
    for at, (first, count) in enumerate(CHUNKS):
        value = jnp.dot(own[at][...], w_own[...], preferred_element_type=F32)
        value += jnp.dot(near[at][...], w_near[...], preferred_element_type=F32)
        value += jnp.dot(far[at][...], w_far[...], preferred_element_type=F32)
        value = value.astype(BF16)
        for shift, out in enumerate(outs):

            @pl.when(pl.program_id(0) == shift)
            def _():
                out[pl.ds(first * BLK, count * BLK), :] = value


def project(info, own, partner, weight, near, far, part):
    tile = weight.shape[1] // HEADS // PARTS
    keep = weight.shape[0] // 2
    rows = RANK_BLOCKS * BLK
    high = [count * BLK for _, count in CHUNKS]

    def target(s, info):
        return lax.rem(info[1] + s, 4)

    def other_tile(s, info):
        return (0, target(s, info) * PARTS + part)

    return pl.pallas_call(
        project_kernel,
        grid_spec=pltpu.PrefetchScalarGridSpec(
            num_scalar_prefetch=1,
            grid=(4,),
            in_specs=[pl.BlockSpec((h, WIDE), lambda s, info: (0, 0)) for h in high]
            + [pl.BlockSpec((h, keep), lambda s, info: (0, info[2])) for h in high]
            + [pl.BlockSpec((h, keep), lambda s, info: (0, 1 - info[2])) for h in high]
            + [
                pl.BlockSpec(
                    (WIDE, tile),
                    lambda s, info: (0, (info[0] * 4 + target(s, info)) * PARTS + part),
                ),
                pl.BlockSpec((keep, tile), other_tile),
                pl.BlockSpec((keep, tile), other_tile),
            ],
            out_specs=[pl.BlockSpec((rows, tile), lambda s, info: (0, 0))] * 4,
        ),
        out_shape=[jax.ShapeDtypeStruct((rows, tile), BF16)] * 4,
        compiler_params=pltpu.CompilerParams(vmem_limit_bytes=VMEM),
        cost_estimate=pl.CostEstimate(
            flops=2 * rows * 2 * WIDE * 4 * tile,
            bytes_accessed=2 * WIDE * 4 * tile * 2 + rows * WIDE * 8,
            transcendentals=0,
        ),
        name="project",
    )(info, *own, *partner, *partner, weight, near, far)


def local(
    queries, query_scale, keys, key_scale, values, value_scale, block_mask, out_weight, out_scale
):
    rank = lax.axis_index("ctx").astype(jnp.int32)
    head = lax.axis_index("head").astype(jnp.int32)
    place = jnp.stack([rank // 2, rank % 2, rank * RANK_BLOCKS])
    info = jnp.stack([head // 4, head % 4, rank % 2])
    packed = pack(keys, key_scale, values, value_scale)
    beside = lax.ppermute(packed, "ctx", [(i, i ^ 2) for i in range(2 * CHIPS)])
    cut = cut_weights(out_weight, rank % 2, head // 4)
    cut, beside = lax.optimization_barrier((cut, beside))
    near = lax.ppermute(cut, ("ctx", "head"), across_y())
    first_kv = with_core(along_x(packed))
    state = attend(
        place, block_mask, queries, query_scale, *first_kv, (0, RANK_BLOCKS), None
    )
    later, state = lax.optimization_barrier((along_x(beside), state))
    second_kv = with_core(later)
    own, partner = [], []
    for chunk in CHUNKS:
        rows = attend(place, block_mask, queries, query_scale, *second_kv, chunk, state)
        if not own:
            near, rows = lax.optimization_barrier((near, rows))
            far = lax.ppermute(near, "ctx", CORE_SWAP)
        own.append(rows)
        partner.append(lax.ppermute(rows, "head", [(i, i ^ 4) for i in range(HEADS)]))
    parts = []
    for part in range(PARTS):
        sums = project(info, own, partner, out_weight, near, far, part)
        total = sums[0].astype(F32)
        for shift in range(1, 4):
            pairs = [(i, i // 4 * 4 + (i + shift) % 4) for i in range(HEADS)]
            total += lax.ppermute(sums[shift], "head", pairs).astype(F32)
        parts.append(total)
    return (jnp.concatenate(parts, axis=1) * out_scale[None, :]).astype(BF16)


def solution(mesh):
    return jax.shard_map(
        local,
        mesh=mesh,
        in_specs=(
            P("ctx", "head"),
            P("ctx", "head"),
            P("ctx", "head"),
            P("ctx", "head"),
            P("ctx", "head"),
            P("ctx", "head"),
            P(),
            P("head", None),
            P("head"),
        ),
        out_specs=P("ctx", "head"),
        check_vma=False,
    )
```

```python
import functools
import math

import jax
import jax.numpy as jnp
from jax import lax
from jax.experimental import pallas as pl
from jax.experimental.pallas import tpu as pltpu
from jax.sharding import PartitionSpec as P

HD = 128
GROUP = 8
BLK = 128
RANK_BLOCKS = 3
CHIPS = 8
DEPTH = 4
HEADS = 8
WIDE = GROUP * HD
QSCALE = math.log2(math.e) / math.sqrt(HD)
F32 = jnp.float32
BF16 = jnp.bfloat16
CHUNKS = ((0, 1), (1, 1), (2, 1))
VMEM = 56 << 20
PARTS = 2


def fold_blocks(count, causal, kv, qt, qrow, top, total, accum):
    keys = jnp.concatenate([kv[b, :, :HD] for b in range(count)], axis=0)
    vals_t = jnp.concatenate([kv[b, :, HD:] for b in range(count)], axis=1)
    span = 2 * BLK
    steps = WIDE // span
    raws = [
        jnp.dot(keys, qt[:, pl.ds(step * span, span)], preferred_element_type=F32)
        for step in range(steps)
    ]
    for step in range(steps):
        cols = pl.ds(step * span, span)
        scores = raws[step] * qrow[:, cols]
        if causal:
            key_at = lax.broadcasted_iota(jnp.int32, (BLK, span), 0)
            row_at = lax.broadcasted_iota(jnp.int32, (BLK, span), 1) % BLK
            own = jnp.where(key_at <= row_at, scores[:BLK], -jnp.inf)
            scores = jnp.concatenate([own, scores[BLK:]], axis=0) if count > 1 else own
            new_top = jnp.max(scores, axis=0, keepdims=True)
            expo = jnp.exp2(scores - new_top)
            total[:, cols] = jnp.sum(expo, axis=0, keepdims=True)
            accum[:, cols] = jnp.dot(vals_t, expo.astype(BF16), preferred_element_type=F32)
        else:
            old_top = top[:, cols]
            new_top = jnp.maximum(old_top, jnp.max(scores, axis=0, keepdims=True))
            expo = jnp.exp2(scores - new_top)
            decay = jnp.exp2(old_top - new_top)
            total[:, cols] = total[:, cols] * decay + jnp.sum(expo, axis=0, keepdims=True)
            accum[:, cols] = accum[:, cols] * decay + jnp.dot(
                vals_t, expo.astype(BF16), preferred_element_type=F32
            )
        top[:, cols] = new_top


def attend_rows(
    first, place, mask, q_ref, qs_ref, mine, other, kv, qt, qrow, top, total, accum, todo, sems
):
    chip, core = place[0], place[1]
    row_block = place[2] + pl.program_id(0)
    column = lax.rem(chip, 2) if first else 1 - lax.rem(chip, 2)
    base = 1 if first else 0

    def fetch(block, slot, at):
        owner = block // RANK_BLOCKS
        index = (chip // 2 - owner // 4) * RANK_BLOCKS + block % RANK_BLOCKS
        for same, source in ((True, mine), (False, other)):

            @pl.when((owner % 2 == core) == same)
            def _():
                pltpu.make_async_copy(source.at[index], kv.at[slot, at], sems.at[slot, at]).start()

    def arrive(slot, at):
        pltpu.make_async_copy(mine.at[0], kv.at[slot, at], sems.at[slot, at]).wait()

    if first:
        fetch(row_block, 0, 0)

    def list_block(block, count):
        todo[count] = block
        wanted = lax.rem(block // (2 * RANK_BLOCKS), 2) == column
        return count + jnp.where(wanted, mask[row_block, block], 0)

    count = lax.fori_loop(0, row_block, list_block, jnp.int32(0))
    rest = count % DEPTH
    full = count // DEPTH
    for at in range(DEPTH - 1):

        @pl.when(at < rest)
        def _():
            fetch(todo[at], 0, at + base)

    def fetch_group(step, slot):
        for at in range(DEPTH):
            fetch(todo[rest + step * DEPTH + at], slot, at)

    @pl.when(full > 0)
    def _():
        fetch_group(0, 1)

    scale = qs_ref[...].astype(F32) * QSCALE
    for head in range(GROUP):
        cols = pl.ds(head * HD, HD)
        qt[:, cols] = q_ref[:, cols].T
        qrow[:, cols] = scale[head : head + 1]

    state = (qt, qrow, top, total, accum)
    if first:
        arrive(0, 0)
    for extra in range(1 - base, DEPTH):

        @pl.when(rest == extra)
        def _():
            for at in range(extra):
                arrive(0, at + base)
            fold_blocks(extra + base, first, kv.at[0], *state)

    @pl.loop(0, full)
    def _(step):
        slot = (step + 1) % 2

        @pl.when(step + 1 < full)
        def _():
            fetch_group(step + 1, 1 - slot)

        for at in range(DEPTH):
            arrive(slot, at)
        fold_blocks(DEPTH, False, kv.at[slot], *state)


def first_kernel(
    place, mask, q_ref, qs_ref, mine, other, top, total, accum, kv, qt, qrow, todo, sems
):
    rows = (place, mask, q_ref, qs_ref, mine, other, kv, qt, qrow)
    attend_rows(True, *rows, top.at[0], total.at[0], accum.at[0], todo, sems)


def second_kernel(
    place, mask, q_ref, qs_ref, mine, other, top_in, total_in, accum_in, o_ref,
    kv, qt, qrow, top, total, accum, todo, sems,
):
    top[...] = top_in[0]
    total[...] = total_in[0]
    accum[...] = accum_in[0]
    rows = (place, mask, q_ref, qs_ref, mine, other, kv, qt, qrow)
    attend_rows(False, *rows, top, total, accum, todo, sems)
    for head in range(GROUP):
        cols = pl.ds(head * HD, HD)
        o_ref[:, cols] = (accum[:, cols] * (1.0 / total[:, cols])).astype(BF16).T


def attend(place, mask, queries, query_scale, mine, other, chunk, state):
    first, count = chunk
    blocks = mask.shape[0]
    smem = pl.BlockSpec(memory_space=pltpu.SMEM)
    hbm = pl.BlockSpec(memory_space=pl.ANY)
    in_specs = [
        smem,
        smem,
        pl.BlockSpec((BLK, WIDE), lambda i: (first + i, 0)),
        pl.BlockSpec((GROUP, BLK), lambda i: (0, first + i)),
        hbm,
        hbm,
    ]
    row = pltpu.VMEM((1, WIDE), F32)
    held = [
        pl.BlockSpec((1, 1, WIDE), lambda i: (first + i, 0, 0)),
        pl.BlockSpec((1, 1, WIDE), lambda i: (first + i, 0, 0)),
        pl.BlockSpec((1, HD, WIDE), lambda i: (first + i, 0, 0)),
    ]
    kv = [pltpu.VMEM((2, DEPTH, BLK, 2 * HD), BF16), pltpu.VMEM((HD, WIDE), BF16), row]
    tail = [pltpu.SMEM((blocks,), jnp.int32), pltpu.SemaphoreType.DMA((2, DEPTH))]
    common = dict(
        grid=(count,),
        compiler_params=pltpu.CompilerParams(vmem_limit_bytes=VMEM),
        cost_estimate=pl.CostEstimate(
            flops=count * BLK * WIDE * 4 * 2500,
            bytes_accessed=count * blocks * BLK * HD * 2,
            transcendentals=count * BLK * GROUP * 2500,
        ),
    )
    args = (
        place + jnp.array([0, 0, first], jnp.int32),
        mask,
        queries,
        query_scale.T,
        mine,
        other,
    )
    if state is None:
        return pl.pallas_call(
            first_kernel,
            in_specs=in_specs,
            out_specs=held,
            out_shape=[
                jax.ShapeDtypeStruct((count, 1, WIDE), F32),
                jax.ShapeDtypeStruct((count, 1, WIDE), F32),
                jax.ShapeDtypeStruct((count, HD, WIDE), F32),
            ],
            scratch_shapes=kv + tail,
            name="attend_first",
            **common,
        )(*args)
    return pl.pallas_call(
        second_kernel,
        in_specs=in_specs + held,
        out_specs=pl.BlockSpec((BLK, WIDE), lambda i: (i, 0)),
        out_shape=jax.ShapeDtypeStruct((count * BLK, WIDE), BF16),
        scratch_shapes=kv + [row, row, pltpu.VMEM((HD, WIDE), F32)] + tail,
        name="attend_second",
        **common,
    )(*args, *state)


def pack_kernel(keys, key_scale, values, value_scale, packed):
    for block in range(RANK_BLOCKS):
        rows = pl.ds(block * BLK, BLK)
        by_row = jnp.broadcast_to(key_scale[:, rows].astype(F32), (HD, BLK)).T
        packed[block, :, :HD] = (keys[rows].astype(F32) * by_row).astype(BF16)
        turned = values[rows].T.astype(F32) * value_scale[:, rows].astype(F32)
        packed[block, :, HD:] = turned.astype(BF16)


def pack(keys, key_scale, values, value_scale):
    vmem = pl.BlockSpec(memory_space=pltpu.VMEM)
    return pl.pallas_call(
        pack_kernel,
        in_specs=[vmem] * 4,
        out_specs=vmem,
        out_shape=jax.ShapeDtypeStruct((RANK_BLOCKS, BLK, 2 * HD), BF16),
        name="pack",
    )(keys, key_scale.T, values, value_scale.T)


def cut_kernel(info, weight, cut, stage, in_sems, out_sems):
    pieces, high, tile = cut.shape
    source = pl.ds(pl.multiple_of(info[2] * high, high), high)

    def copies(piece):
        first = pl.multiple_of(((1 - info[0]) * pieces + piece) * tile, tile)
        return (
            pltpu.make_async_copy(
                weight.at[source, pl.ds(first, tile)], stage.at[piece], in_sems.at[piece]
            ),
            pltpu.make_async_copy(stage.at[piece], cut.at[piece], out_sems.at[piece]),
        )

    loads = [copies(piece) for piece in range(pieces)]
    for load, _ in loads:
        load.start()
    for load, store in loads:
        load.wait()
        store.start()
    for _, store in loads:
        store.wait()


def cut_weights(info, weight):
    hbm = pl.BlockSpec(memory_space=pltpu.HBM)
    pieces = 4 * PARTS
    shape = (pieces, weight.shape[0] // 2, weight.shape[1] // 2 // pieces)
    return pl.pallas_call(
        cut_kernel,
        in_specs=[pl.BlockSpec(memory_space=pltpu.SMEM), hbm],
        out_specs=hbm,
        out_shape=jax.ShapeDtypeStruct(shape, BF16),
        scratch_shapes=[
            pltpu.VMEM(shape, BF16),
            pltpu.SemaphoreType.DMA((pieces,)),
            pltpu.SemaphoreType.DMA((pieces,)),
        ],
        compiler_params=pltpu.CompilerParams(vmem_limit_bytes=VMEM),
        cost_estimate=pl.CostEstimate(flops=0, bytes_accessed=16 << 20, transcendentals=0),
        name="cut",
    )(info, weight)


CORE_SWAP = [(i, i ^ 1) for i in range(2 * CHIPS)]


def along_x(block):
    got = [block]
    for shift in range(1, 4):
        pairs = [(4 * x + i, 4 * (x + shift) + i) for x in range(4 - shift) for i in range(4)]
        got.append(lax.ppermute(block, "ctx", pairs))
    return got


def with_core(got):
    mine = jnp.concatenate(got, axis=0)
    return mine, lax.ppermute(mine, "ctx", CORE_SWAP)


def across_y():
    pairs = []
    for x in range(4):
        for y in range(4):
            for core in range(2):
                for z in range(4):
                    far = (y + (1 if core == 0 else 3)) % 4
                    start = ((x * 2 + y // 2) * 2 + core) * HEADS + (y % 2) * 4 + z
                    end = ((x * 2 + far // 2) * 2 + core) * HEADS + (far % 2) * 4 + z
                    pairs.append((start, end))
    return pairs


def own_kernel(info, *refs):
    chunks = len(CHUNKS)
    own = refs[:chunks]
    weight, out, left, held, sems = refs[chunks:]
    tile = held.shape[2]

    def copies(shift):
        target = lax.rem(info[1] + shift, 4)
        mine = pl.ds(pl.multiple_of((info[0] * 4 + target) * tile, tile), tile)
        yield pltpu.make_async_copy(weight.at[:, mine], held.at[shift], sems.at[shift])

    for shift in range(4):
        for copy in copies(shift):
            copy.start()
    for at, (first, count) in enumerate(CHUNKS):
        left[pl.ds(first * BLK, count * BLK), :] = own[at][...]
    for shift in range(4):
        for copy in copies(shift):
            copy.wait()
        for at in range(RANK_BLOCKS):
            rows = pl.ds(at * BLK, BLK)
            value = jnp.dot(left[rows], held[shift], preferred_element_type=F32)
            width = out.shape[3]
            for part in range(PARTS):
                half = value[:, part * width : (part + 1) * width]
                out[part, shift, rows] = half.astype(BF16)


def project_own(info, own, weight):
    tile = weight.shape[1] // HEADS
    rows = RANK_BLOCKS * BLK
    vmem = pl.BlockSpec(memory_space=pltpu.VMEM)
    return pl.pallas_call(
        own_kernel,
        in_specs=[pl.BlockSpec(memory_space=pltpu.SMEM)]
        + [vmem] * len(CHUNKS)
        + [pl.BlockSpec(memory_space=pltpu.HBM)],
        out_specs=vmem,
        out_shape=jax.ShapeDtypeStruct((PARTS, 4, rows, tile // PARTS), BF16),
        scratch_shapes=[
            pltpu.VMEM((rows, WIDE), BF16),
            pltpu.VMEM((4, weight.shape[0], tile), BF16),
            pltpu.SemaphoreType.DMA((4,)),
        ],
        compiler_params=pltpu.CompilerParams(vmem_limit_bytes=VMEM),
        cost_estimate=pl.CostEstimate(
            flops=2 * rows * WIDE * 4 * tile,
            bytes_accessed=WIDE * 4 * tile * 2 + rows * WIDE * 10,
            transcendentals=0,
        ),
        name="project_own",
    )(info, *own, weight)


ORDER = (2, 1, 3, 0)


def partner_kernel(part, info, *refs):
    chunks = len(CHUNKS)
    partner = refs[:chunks]
    base, near, far = refs[chunks : chunks + 3]
    outs = refs[chunks + 3 :][:4]
    left, held, begun, sems = refs[-4:]
    keep = near.shape[1]

    def copies(at):
        shift = ORDER[at]
        piece = lax.rem(info[1] + shift, 4) * PARTS + part
        for which, source in ((0, near), (1, far)):
            half = lax.rem(info[2] + which, 2)
            rows = pl.ds(pl.multiple_of(half * keep, keep), keep)
            yield pltpu.make_async_copy(
                source.at[piece], held.at[shift, rows], sems.at[shift, which]
            )
        yield pltpu.make_async_copy(base.at[part, shift], begun.at[shift], sems.at[shift, 2])

    for at in range(2):
        for copy in copies(at):
            copy.start()
    for at, (first, count) in enumerate(CHUNKS):
        left[pl.ds(first * BLK, count * BLK), :] = partner[at][...]
    for at, shift in enumerate(ORDER):
        for copy in copies(at):
            copy.wait()
        if at + 2 < len(ORDER):
            for copy in copies(at + 2):
                copy.start()
        for block in range(RANK_BLOCKS):
            rows = pl.ds(block * BLK, BLK)
            value = jnp.dot(left[rows], held[shift], preferred_element_type=F32)
            outs[shift][rows] = (value + begun[shift, rows].astype(F32)).astype(BF16)


def project_partner(info, partner, base, near, far, part):
    _, _, rows, tile = base.shape
    vmem = pl.BlockSpec(memory_space=pltpu.VMEM)
    hbm = pl.BlockSpec(memory_space=pltpu.HBM)
    return pl.pallas_call(
        functools.partial(partner_kernel, part),
        in_specs=[pl.BlockSpec(memory_space=pltpu.SMEM)] + [vmem] * len(CHUNKS) + [hbm] * 3,
        out_specs=[vmem] * 4,
        out_shape=[jax.ShapeDtypeStruct((rows, tile), BF16)] * 4,
        scratch_shapes=[
            pltpu.VMEM((rows, WIDE), BF16),
            pltpu.VMEM((4, WIDE, tile), BF16),
            pltpu.VMEM((4, rows, tile), BF16),
            pltpu.SemaphoreType.DMA((4, 3)),
        ],
        compiler_params=pltpu.CompilerParams(vmem_limit_bytes=VMEM),
        cost_estimate=pl.CostEstimate(
            flops=2 * rows * WIDE * 4 * tile,
            bytes_accessed=WIDE * 4 * tile * 2 + rows * WIDE * 8,
            transcendentals=0,
        ),
        name="project_partner",
    )(info, *partner, base, near, far)


def ring(block, step):
    return lax.ppermute(block, "head", [(i, i // 4 * 4 + (i + step) % 4) for i in range(HEADS)])


def sum_over_z(sums, clockwise):
    own, ahead, across, behind = sums
    step = 1 if clockwise else -1
    first, second = (ahead, behind) if clockwise else (behind, ahead)
    passed = ring(across, step)
    direct = ring(second, -step)
    joined = ring((first.astype(F32) + passed.astype(F32)).astype(BF16), step)
    return own.astype(F32) + direct.astype(F32) + joined.astype(F32)


def local(
    queries, query_scale, keys, key_scale, values, value_scale, block_mask, out_weight, out_scale
):
    rank = lax.axis_index("ctx").astype(jnp.int32)
    head = lax.axis_index("head").astype(jnp.int32)
    place = jnp.stack([rank // 2, rank % 2, rank * RANK_BLOCKS])
    info = jnp.stack([head // 4, head % 4, rank % 2])
    packed = pack(keys, key_scale, values, value_scale)
    cut = cut_weights(info, out_weight)
    beside = lax.ppermute(packed, "ctx", [(i, i ^ 2) for i in range(2 * CHIPS)])
    along = along_x(packed)
    cut, beside = lax.optimization_barrier((cut, beside))
    near = lax.ppermute(cut, ("ctx", "head"), across_y())
    first_kv = with_core(along)
    state = attend(
        place, block_mask, queries, query_scale, *first_kv, (0, RANK_BLOCKS), None
    )
    later, state = lax.optimization_barrier((along_x(beside), state))
    second_kv = with_core(later)
    own, partner = [], []
    for at, chunk in enumerate(CHUNKS):
        rows = attend(place, block_mask, queries, query_scale, *second_kv, chunk, state)
        rows, state = lax.optimization_barrier((rows, state))
        own.append(rows)
        partner.append(lax.ppermute(rows, "head", [(i, i ^ 4) for i in range(HEADS)]))
        if at == 0:
            near, state = lax.optimization_barrier((near, state))
            far = lax.ppermute(near, "ctx", CORE_SWAP)
        if at == 1:
            partner[0], state = lax.optimization_barrier((partner[0], state))
    own, partner[1] = lax.optimization_barrier((own, partner[1]))
    base = project_own(info, own, out_weight)
    parts = []
    for part in range(PARTS):
        sums = project_partner(info, partner, base, near, far, part)
        parts.append(sum_over_z(sums, part % 2 == 0))
    return (jnp.concatenate(parts, axis=1) * out_scale[None, :]).astype(BF16)


def solution(mesh):
    return jax.shard_map(
        local,
        mesh=mesh,
        in_specs=(
            P("ctx", "head"),
            P("ctx", "head"),
            P("ctx", "head"),
            P("ctx", "head"),
            P("ctx", "head"),
            P("ctx", "head"),
            P(),
            P("head", None),
            P("head"),
        ),
        out_specs=P("ctx", "head"),
        check_vma=False,
    )
```

```python
import functools
import math

import jax
import jax.numpy as jnp
from jax import lax
from jax.experimental import pallas as pl
from jax.experimental.pallas import tpu as pltpu
from jax.sharding import PartitionSpec as P

HD = 128
GROUP = 8
BLK = 128
RANK_BLOCKS = 3
CHIPS = 8
DEPTH = 4
HEADS = 8
WIDE = GROUP * HD
QSCALE = math.log2(math.e) / math.sqrt(HD)
F32 = jnp.float32
BF16 = jnp.bfloat16
CHUNKS = ((0, 1), (1, 1), (2, 1))
VMEM = 48 << 20
PARTS = 2


def fold_blocks(count, causal, kv, qt, qrow, top, total, accum):
    keys = jnp.concatenate([kv[b, :, :HD] for b in range(count)], axis=0)
    vals_t = jnp.concatenate([kv[b, :, HD:] for b in range(count)], axis=1)
    span = 2 * BLK
    steps = WIDE // span
    raws = [
        jnp.dot(keys, qt[:, pl.ds(step * span, span)], preferred_element_type=F32)
        for step in range(steps)
    ]
    for step in range(steps):
        cols = pl.ds(step * span, span)
        scores = raws[step] * qrow[:, cols]
        if causal:
            key_at = lax.broadcasted_iota(jnp.int32, (BLK, span), 0)
            row_at = lax.broadcasted_iota(jnp.int32, (BLK, span), 1) % BLK
            own = jnp.where(key_at <= row_at, scores[:BLK], -jnp.inf)
            scores = jnp.concatenate([own, scores[BLK:]], axis=0) if count > 1 else own
            new_top = jnp.max(scores, axis=0, keepdims=True)
            expo = jnp.exp2(scores - new_top)
            total[:, cols] = jnp.sum(expo, axis=0, keepdims=True)
            accum[:, cols] = jnp.dot(vals_t, expo.astype(BF16), preferred_element_type=F32)
        else:
            old_top = top[:, cols]
            new_top = jnp.maximum(old_top, jnp.max(scores, axis=0, keepdims=True))
            expo = jnp.exp2(scores - new_top)
            decay = jnp.exp2(old_top - new_top)
            total[:, cols] = total[:, cols] * decay + jnp.sum(expo, axis=0, keepdims=True)
            accum[:, cols] = accum[:, cols] * decay + jnp.dot(
                vals_t, expo.astype(BF16), preferred_element_type=F32
            )
        top[:, cols] = new_top


def attend_rows(
    first, place, mask, q_ref, qs_ref, mine, other, kv, qt, qrow, top, total, accum, todo, sems
):
    chip, core = place[0], place[1]
    row_block = place[2] + pl.program_id(0)
    column = lax.rem(chip, 2) if first else 1 - lax.rem(chip, 2)
    base = 1 if first else 0

    def fetch(block, slot, at):
        owner = block // RANK_BLOCKS
        index = (chip // 2 - owner // 4) * RANK_BLOCKS + block % RANK_BLOCKS
        for same, source in ((True, mine), (False, other)):

            @pl.when((owner % 2 == core) == same)
            def _():
                pltpu.make_async_copy(source.at[index], kv.at[slot, at], sems.at[slot, at]).start()

    def arrive(slot, at):
        pltpu.make_async_copy(mine.at[0], kv.at[slot, at], sems.at[slot, at]).wait()

    if first:
        fetch(row_block, 0, 0)

    def list_block(block, count):
        todo[count] = block
        wanted = lax.rem(block // (2 * RANK_BLOCKS), 2) == column
        return count + jnp.where(wanted, mask[row_block, block], 0)

    count = lax.fori_loop(0, row_block, list_block, jnp.int32(0))
    rest = count % DEPTH
    full = count // DEPTH
    for at in range(DEPTH - 1):

        @pl.when(at < rest)
        def _():
            fetch(todo[at], 0, at + base)

    def fetch_group(step, slot):
        for at in range(DEPTH):
            fetch(todo[rest + step * DEPTH + at], slot, at)

    @pl.when(full > 0)
    def _():
        fetch_group(0, 1)

    scale = qs_ref[...].astype(F32) * QSCALE
    for head in range(GROUP):
        cols = pl.ds(head * HD, HD)
        qt[:, cols] = q_ref[:, cols].T
        qrow[:, cols] = scale[head : head + 1]

    state = (qt, qrow, top, total, accum)
    if first:
        arrive(0, 0)
    for extra in range(1 - base, DEPTH):

        @pl.when(rest == extra)
        def _():
            for at in range(extra):
                arrive(0, at + base)
            fold_blocks(extra + base, first, kv.at[0], *state)

    @pl.loop(0, full)
    def _(step):
        slot = (step + 1) % 2

        @pl.when(step + 1 < full)
        def _():
            fetch_group(step + 1, 1 - slot)

        for at in range(DEPTH):
            arrive(slot, at)
        fold_blocks(DEPTH, False, kv.at[slot], *state)


def first_kernel(
    place, mask, q_ref, qs_ref, mine, other, top, total, accum, kv, qt, qrow, todo, sems
):
    rows = (place, mask, q_ref, qs_ref, mine, other, kv, qt, qrow)
    attend_rows(True, *rows, top.at[0], total.at[0], accum.at[0], todo, sems)


def second_kernel(
    place, mask, q_ref, qs_ref, mine, other, top_in, total_in, accum_in, o_ref,
    kv, qt, qrow, top, total, accum, todo, sems,
):
    top[...] = top_in[0]
    total[...] = total_in[0]
    accum[...] = accum_in[0]
    rows = (place, mask, q_ref, qs_ref, mine, other, kv, qt, qrow)
    attend_rows(False, *rows, top, total, accum, todo, sems)
    for head in range(GROUP):
        cols = pl.ds(head * HD, HD)
        o_ref[:, cols] = (accum[:, cols] * (1.0 / total[:, cols])).astype(BF16).T


def attend(place, mask, queries, query_scale, mine, other, chunk, state):
    first, count = chunk
    blocks = mask.shape[0]
    smem = pl.BlockSpec(memory_space=pltpu.SMEM)
    hbm = pl.BlockSpec(memory_space=pl.ANY)
    in_specs = [
        smem,
        smem,
        pl.BlockSpec((BLK, WIDE), lambda i: (first + i, 0)),
        pl.BlockSpec((GROUP, BLK), lambda i: (0, first + i)),
        hbm,
        hbm,
    ]
    row = pltpu.VMEM((1, WIDE), F32)
    held = [
        pl.BlockSpec((1, 1, WIDE), lambda i: (first + i, 0, 0)),
        pl.BlockSpec((1, 1, WIDE), lambda i: (first + i, 0, 0)),
        pl.BlockSpec((1, HD, WIDE), lambda i: (first + i, 0, 0)),
    ]
    kv = [pltpu.VMEM((2, DEPTH, BLK, 2 * HD), BF16), pltpu.VMEM((HD, WIDE), BF16), row]
    tail = [pltpu.SMEM((blocks,), jnp.int32), pltpu.SemaphoreType.DMA((2, DEPTH))]
    common = dict(
        grid=(count,),
        compiler_params=pltpu.CompilerParams(vmem_limit_bytes=VMEM),
        cost_estimate=pl.CostEstimate(
            flops=count * BLK * WIDE * 4 * 2500,
            bytes_accessed=count * blocks * BLK * HD * 2,
            transcendentals=count * BLK * GROUP * 2500,
        ),
    )
    args = (
        place + jnp.array([0, 0, first], jnp.int32),
        mask,
        queries,
        query_scale.T,
        mine,
        other,
    )
    if state is None:
        return pl.pallas_call(
            first_kernel,
            in_specs=in_specs,
            out_specs=held,
            out_shape=[
                jax.ShapeDtypeStruct((count, 1, WIDE), F32),
                jax.ShapeDtypeStruct((count, 1, WIDE), F32),
                jax.ShapeDtypeStruct((count, HD, WIDE), F32),
            ],
            scratch_shapes=kv + tail,
            name="attend_first",
            **common,
        )(*args)
    return pl.pallas_call(
        second_kernel,
        in_specs=in_specs + held,
        out_specs=pl.BlockSpec((BLK, WIDE), lambda i: (i, 0)),
        out_shape=jax.ShapeDtypeStruct((count * BLK, WIDE), BF16),
        scratch_shapes=kv + [row, row, pltpu.VMEM((HD, WIDE), F32)] + tail,
        name="attend_second",
        **common,
    )(*args, *state)


def pack_kernel(keys, key_scale, values, value_scale, packed):
    for block in range(RANK_BLOCKS):
        rows = pl.ds(block * BLK, BLK)
        by_row = jnp.broadcast_to(key_scale[:, rows].astype(F32), (HD, BLK)).T
        packed[block, :, :HD] = (keys[rows].astype(F32) * by_row).astype(BF16)
        turned = values[rows].T.astype(F32) * value_scale[:, rows].astype(F32)
        packed[block, :, HD:] = turned.astype(BF16)


def pack(keys, key_scale, values, value_scale):
    vmem = pl.BlockSpec(memory_space=pltpu.VMEM)
    return pl.pallas_call(
        pack_kernel,
        in_specs=[vmem] * 4,
        out_specs=vmem,
        out_shape=jax.ShapeDtypeStruct((RANK_BLOCKS, BLK, 2 * HD), BF16),
        name="pack",
    )(keys, key_scale.T, values, value_scale.T)


def cut_kernel(info, weight, cut, stage, in_sems, out_sems):
    pieces, high, tile = cut.shape
    source = pl.ds(pl.multiple_of(info[2] * high, high), high)

    def copies(piece):
        first = pl.multiple_of(((1 - info[0]) * pieces + piece) * tile, tile)
        return (
            pltpu.make_async_copy(
                weight.at[source, pl.ds(first, tile)], stage.at[piece], in_sems.at[piece]
            ),
            pltpu.make_async_copy(stage.at[piece], cut.at[piece], out_sems.at[piece]),
        )

    loads = [copies(piece) for piece in range(pieces)]
    for load, _ in loads:
        load.start()
    for load, store in loads:
        load.wait()
        store.start()
    for _, store in loads:
        store.wait()


def cut_weights(info, weight):
    hbm = pl.BlockSpec(memory_space=pltpu.HBM)
    pieces = 4 * PARTS
    shape = (pieces, weight.shape[0] // 2, weight.shape[1] // 2 // pieces)
    return pl.pallas_call(
        cut_kernel,
        in_specs=[pl.BlockSpec(memory_space=pltpu.SMEM), hbm],
        out_specs=hbm,
        out_shape=jax.ShapeDtypeStruct(shape, BF16),
        scratch_shapes=[
            pltpu.VMEM(shape, BF16),
            pltpu.SemaphoreType.DMA((pieces,)),
            pltpu.SemaphoreType.DMA((pieces,)),
        ],
        compiler_params=pltpu.CompilerParams(vmem_limit_bytes=VMEM),
        cost_estimate=pl.CostEstimate(flops=0, bytes_accessed=16 << 20, transcendentals=0),
        name="cut",
    )(info, weight)


CORE_SWAP = [(i, i ^ 1) for i in range(2 * CHIPS)]


def along_x(block):
    got = [block]
    for shift in range(1, 4):
        pairs = [(4 * x + i, 4 * (x + shift) + i) for x in range(4 - shift) for i in range(4)]
        got.append(lax.ppermute(block, "ctx", pairs))
    return got


def with_core(got):
    mine = jnp.concatenate(got, axis=0)
    return mine, lax.ppermute(mine, "ctx", CORE_SWAP)


def across_y():
    pairs = []
    for x in range(4):
        for y in range(4):
            for core in range(2):
                for z in range(4):
                    far = (y + (1 if core == 0 else 3)) % 4
                    start = ((x * 2 + y // 2) * 2 + core) * HEADS + (y % 2) * 4 + z
                    end = ((x * 2 + far // 2) * 2 + core) * HEADS + (far % 2) * 4 + z
                    pairs.append((start, end))
    return pairs


def own_kernel(info, *refs):
    chunks = len(CHUNKS)
    own = refs[:chunks]
    weight, out, left, held, sems = refs[chunks:]
    tile = held.shape[2]

    def copies(shift):
        target = lax.rem(info[1] + shift, 4)
        mine = pl.ds(pl.multiple_of((info[0] * 4 + target) * tile, tile), tile)
        yield pltpu.make_async_copy(weight.at[:, mine], held.at[shift], sems.at[shift])

    for shift in range(4):
        for copy in copies(shift):
            copy.start()
    for at, (first, count) in enumerate(CHUNKS):
        left[pl.ds(first * BLK, count * BLK), :] = own[at][...]
    for shift in range(4):
        for copy in copies(shift):
            copy.wait()
        for at in range(RANK_BLOCKS):
            rows = pl.ds(at * BLK, BLK)
            value = jnp.dot(left[rows], held[shift], preferred_element_type=F32)
            width = out.shape[3]
            for part in range(PARTS):
                half = value[:, part * width : (part + 1) * width]
                out[part, shift, rows] = half.astype(BF16)


def project_own(info, own, weight):
    tile = weight.shape[1] // HEADS
    rows = RANK_BLOCKS * BLK
    vmem = pl.BlockSpec(memory_space=pltpu.VMEM)
    return pl.pallas_call(
        own_kernel,
        in_specs=[pl.BlockSpec(memory_space=pltpu.SMEM)]
        + [vmem] * len(CHUNKS)
        + [pl.BlockSpec(memory_space=pltpu.HBM)],
        out_specs=vmem,
        out_shape=jax.ShapeDtypeStruct((PARTS, 4, rows, tile // PARTS), BF16),
        scratch_shapes=[
            pltpu.VMEM((rows, WIDE), BF16),
            pltpu.VMEM((4, weight.shape[0], tile), BF16),
            pltpu.SemaphoreType.DMA((4,)),
        ],
        compiler_params=pltpu.CompilerParams(vmem_limit_bytes=VMEM),
        cost_estimate=pl.CostEstimate(
            flops=2 * rows * WIDE * 4 * tile,
            bytes_accessed=WIDE * 4 * tile * 2 + rows * WIDE * 10,
            transcendentals=0,
        ),
        name="project_own",
    )(info, *own, weight)


ORDER = (2, 1, 3, 0)


def partner_kernel(part, info, *refs):
    chunks = len(CHUNKS)
    partner = refs[:chunks]
    base, near, far = refs[chunks : chunks + 3]
    outs = refs[chunks + 3 :][:4]
    left, held, begun, sems = refs[-4:]
    keep = near.shape[1]

    def copies(at):
        shift = ORDER[at]
        piece = lax.rem(info[1] + shift, 4) * PARTS + part
        for which, source in ((0, near), (1, far)):
            half = lax.rem(info[2] + which, 2)
            rows = pl.ds(pl.multiple_of(half * keep, keep), keep)
            yield pltpu.make_async_copy(
                source.at[piece], held.at[shift, rows], sems.at[shift, which]
            )
        yield pltpu.make_async_copy(base.at[part, shift], begun.at[shift], sems.at[shift, 2])

    for at in range(2):
        for copy in copies(at):
            copy.start()
    for at, (first, count) in enumerate(CHUNKS):
        left[pl.ds(first * BLK, count * BLK), :] = partner[at][...]
    for at, shift in enumerate(ORDER):
        for copy in copies(at):
            copy.wait()
        if at + 2 < len(ORDER):
            for copy in copies(at + 2):
                copy.start()
        for block in range(RANK_BLOCKS):
            rows = pl.ds(block * BLK, BLK)
            value = jnp.dot(left[rows], held[shift], preferred_element_type=F32)
            outs[shift][rows] = (value + begun[shift, rows].astype(F32)).astype(BF16)


def project_partner(info, partner, base, near, far, part):
    _, _, rows, tile = base.shape
    vmem = pl.BlockSpec(memory_space=pltpu.VMEM)
    hbm = pl.BlockSpec(memory_space=pltpu.HBM)
    return pl.pallas_call(
        functools.partial(partner_kernel, part),
        in_specs=[pl.BlockSpec(memory_space=pltpu.SMEM)] + [vmem] * len(CHUNKS) + [hbm] * 3,
        out_specs=[vmem] * 4,
        out_shape=[jax.ShapeDtypeStruct((rows, tile), BF16)] * 4,
        scratch_shapes=[
            pltpu.VMEM((rows, WIDE), BF16),
            pltpu.VMEM((4, WIDE, tile), BF16),
            pltpu.VMEM((4, rows, tile), BF16),
            pltpu.SemaphoreType.DMA((4, 3)),
        ],
        compiler_params=pltpu.CompilerParams(vmem_limit_bytes=20 << 20),
        cost_estimate=pl.CostEstimate(
            flops=2 * rows * WIDE * 4 * tile,
            bytes_accessed=WIDE * 4 * tile * 2 + rows * WIDE * 8,
            transcendentals=0,
        ),
        name="project_partner",
    )(info, *partner, base, near, far)


def ring(block, step):
    return lax.ppermute(block, "head", [(i, i // 4 * 4 + (i + step) % 4) for i in range(HEADS)])


def sum_over_z(sums, clockwise):
    own, ahead, across, behind = sums
    step = 1 if clockwise else -1
    first, second = (ahead, behind) if clockwise else (behind, ahead)
    passed = ring(across, step)
    direct = ring(second, -step)
    joined = ring((first.astype(F32) + passed.astype(F32)).astype(BF16), step)
    return own.astype(F32) + direct.astype(F32) + joined.astype(F32)


def local(
    queries, query_scale, keys, key_scale, values, value_scale, block_mask, out_weight, out_scale
):
    rank = lax.axis_index("ctx").astype(jnp.int32)
    head = lax.axis_index("head").astype(jnp.int32)
    place = jnp.stack([rank // 2, rank % 2, rank * RANK_BLOCKS])
    info = jnp.stack([head // 4, head % 4, rank % 2])
    packed = pack(keys, key_scale, values, value_scale)
    cut = cut_weights(info, out_weight)
    beside = lax.ppermute(packed, "ctx", [(i, i ^ 2) for i in range(2 * CHIPS)])
    along = along_x(packed)
    cut, beside = lax.optimization_barrier((cut, beside))
    near = lax.ppermute(cut, ("ctx", "head"), across_y())
    along, beside = lax.optimization_barrier((along, beside))
    first_kv = with_core(along)
    state = attend(
        place, block_mask, queries, query_scale, *first_kv, (0, RANK_BLOCKS), None
    )
    later, state = lax.optimization_barrier((along_x(beside), state))
    second_kv = with_core(later)
    own, partner = [], []
    for at, chunk in enumerate(CHUNKS):
        rows = attend(place, block_mask, queries, query_scale, *second_kv, chunk, state)
        rows, state = lax.optimization_barrier((rows, state))
        own.append(rows)
        partner.append(lax.ppermute(rows, "head", [(i, i ^ 4) for i in range(HEADS)]))
    own, partner[:2], near = lax.optimization_barrier((own, partner[:2], near))
    base = project_own(info, own, out_weight)
    far = lax.ppermute(near, "ctx", CORE_SWAP)
    parts = []
    for part in range(PARTS):
        sums = project_partner(info, partner, base, near, far, part)
        parts.append(sum_over_z(sums, part % 2 == 0))
    return (jnp.concatenate(parts, axis=1) * out_scale[None, :]).astype(BF16)


def solution(mesh):
    return jax.shard_map(
        local,
        mesh=mesh,
        in_specs=(
            P("ctx", "head"),
            P("ctx", "head"),
            P("ctx", "head"),
            P("ctx", "head"),
            P("ctx", "head"),
            P("ctx", "head"),
            P(),
            P("head", None),
            P("head"),
        ),
        out_specs=P("ctx", "head"),
        check_vma=False,
    )
```

```python
import functools
import math

import jax
import jax.numpy as jnp
from jax import lax
from jax.experimental import pallas as pl
from jax.experimental.pallas import tpu as pltpu
from jax.sharding import PartitionSpec as P

HD = 128
GROUP = 8
BLK = 128
RANK_BLOCKS = 3
CHIPS = 8
DEPTH = 4
HEADS = 8
WIDE = GROUP * HD
QSCALE = math.log2(math.e) / math.sqrt(HD)
F32 = jnp.float32
BF16 = jnp.bfloat16
CHUNKS = ((0, 1), (1, 1), (2, 1))
VMEM = 48 << 20
PARTS = 2


def fold_blocks(count, causal, kv, qt, qrow, top, total, accum):
    keys = jnp.concatenate([kv[b, :, :HD] for b in range(count)], axis=0)
    vals_t = jnp.concatenate([kv[b, :, HD:] for b in range(count)], axis=1)
    span = 2 * BLK
    steps = WIDE // span
    raws = [
        jnp.dot(keys, qt[:, pl.ds(step * span, span)], preferred_element_type=F32)
        for step in range(steps)
    ]
    for step in range(steps):
        cols = pl.ds(step * span, span)
        scores = raws[step] * qrow[:, cols]
        if causal:
            key_at = lax.broadcasted_iota(jnp.int32, (BLK, span), 0)
            row_at = lax.broadcasted_iota(jnp.int32, (BLK, span), 1) % BLK
            own = jnp.where(key_at <= row_at, scores[:BLK], -jnp.inf)
            scores = jnp.concatenate([own, scores[BLK:]], axis=0) if count > 1 else own
            new_top = jnp.max(scores, axis=0, keepdims=True)
            expo = jnp.exp2(scores - new_top)
            total[:, cols] = jnp.sum(expo, axis=0, keepdims=True)
            accum[:, cols] = jnp.dot(vals_t, expo.astype(BF16), preferred_element_type=F32)
        else:
            old_top = top[:, cols]
            new_top = jnp.maximum(old_top, jnp.max(scores, axis=0, keepdims=True))
            expo = jnp.exp2(scores - new_top)
            decay = jnp.exp2(old_top - new_top)
            total[:, cols] = total[:, cols] * decay + jnp.sum(expo, axis=0, keepdims=True)
            accum[:, cols] = accum[:, cols] * decay + jnp.dot(
                vals_t, expo.astype(BF16), preferred_element_type=F32
            )
        top[:, cols] = new_top


def attend_rows(
    first, place, mask, q_ref, qs_ref, mine, other, kv, qt, qrow, top, total, accum, todo, sems
):
    chip, core = place[0], place[1]
    row_block = place[2] + pl.program_id(0)
    column = lax.rem(chip, 2) if first else 1 - lax.rem(chip, 2)
    base = 1 if first else 0

    def fetch(block, slot, at):
        owner = block // RANK_BLOCKS
        index = (chip // 2 - owner // 4) * RANK_BLOCKS + block % RANK_BLOCKS
        for same, source in ((True, mine), (False, other)):

            @pl.when((owner % 2 == core) == same)
            def _():
                pltpu.make_async_copy(source.at[index], kv.at[slot, at], sems.at[slot, at]).start()

    def arrive(slot, at):
        pltpu.make_async_copy(mine.at[0], kv.at[slot, at], sems.at[slot, at]).wait()

    if first:
        fetch(row_block, 0, 0)

    def list_block(block, count):
        todo[count] = block
        wanted = lax.rem(block // (2 * RANK_BLOCKS), 2) == column
        return count + jnp.where(wanted, mask[row_block, block], 0)

    count = lax.fori_loop(0, row_block, list_block, jnp.int32(0))
    rest = count % DEPTH
    full = count // DEPTH
    for at in range(DEPTH - 1):

        @pl.when(at < rest)
        def _():
            fetch(todo[at], 0, at + base)

    def fetch_group(step, slot):
        for at in range(DEPTH):
            fetch(todo[rest + step * DEPTH + at], slot, at)

    @pl.when(full > 0)
    def _():
        fetch_group(0, 1)

    scale = qs_ref[...].astype(F32) * QSCALE
    for head in range(GROUP):
        cols = pl.ds(head * HD, HD)
        qt[:, cols] = q_ref[:, cols].T
        qrow[:, cols] = scale[head : head + 1]

    state = (qt, qrow, top, total, accum)
    if first:
        arrive(0, 0)
    for extra in range(1 - base, DEPTH):

        @pl.when(rest == extra)
        def _():
            for at in range(extra):
                arrive(0, at + base)
            fold_blocks(extra + base, first, kv.at[0], *state)

    @pl.loop(0, full)
    def _(step):
        slot = (step + 1) % 2

        @pl.when(step + 1 < full)
        def _():
            fetch_group(step + 1, 1 - slot)

        for at in range(DEPTH):
            arrive(slot, at)
        fold_blocks(DEPTH, False, kv.at[slot], *state)


def first_kernel(
    place, mask, q_ref, qs_ref, mine, other, top, total, accum, kv, qt, qrow, todo, sems
):
    rows = (place, mask, q_ref, qs_ref, mine, other, kv, qt, qrow)
    attend_rows(True, *rows, top.at[0], total.at[0], accum.at[0], todo, sems)


def second_kernel(
    place, mask, q_ref, qs_ref, mine, other, top_in, total_in, accum_in, o_ref,
    kv, qt, qrow, top, total, accum, todo, sems,
):
    top[...] = top_in[0]
    total[...] = total_in[0]
    accum[...] = accum_in[0]
    rows = (place, mask, q_ref, qs_ref, mine, other, kv, qt, qrow)
    attend_rows(False, *rows, top, total, accum, todo, sems)
    for head in range(GROUP):
        cols = pl.ds(head * HD, HD)
        o_ref[:, cols] = (accum[:, cols] * (1.0 / total[:, cols])).astype(BF16).T


def attend(place, mask, queries, query_scale, mine, other, chunk, state):
    first, count = chunk
    blocks = mask.shape[0]
    smem = pl.BlockSpec(memory_space=pltpu.SMEM)
    hbm = pl.BlockSpec(memory_space=pl.ANY)
    in_specs = [
        smem,
        smem,
        pl.BlockSpec((BLK, WIDE), lambda i: (first + i, 0)),
        pl.BlockSpec((GROUP, BLK), lambda i: (0, first + i)),
        hbm,
        hbm,
    ]
    row = pltpu.VMEM((1, WIDE), F32)
    held = [
        pl.BlockSpec((1, 1, WIDE), lambda i: (first + i, 0, 0)),
        pl.BlockSpec((1, 1, WIDE), lambda i: (first + i, 0, 0)),
        pl.BlockSpec((1, HD, WIDE), lambda i: (first + i, 0, 0)),
    ]
    kv = [pltpu.VMEM((2, DEPTH, BLK, 2 * HD), BF16), pltpu.VMEM((HD, WIDE), BF16), row]
    tail = [pltpu.SMEM((blocks,), jnp.int32), pltpu.SemaphoreType.DMA((2, DEPTH))]
    common = dict(
        grid=(count,),
        compiler_params=pltpu.CompilerParams(vmem_limit_bytes=VMEM),
        cost_estimate=pl.CostEstimate(
            flops=count * BLK * WIDE * 4 * 2500,
            bytes_accessed=count * blocks * BLK * HD * 2,
            transcendentals=count * BLK * GROUP * 2500,
        ),
    )
    args = (
        place + jnp.array([0, 0, first], jnp.int32),
        mask,
        queries,
        query_scale.T,
        mine,
        other,
    )
    if state is None:
        return pl.pallas_call(
            first_kernel,
            in_specs=in_specs,
            out_specs=held,
            out_shape=[
                jax.ShapeDtypeStruct((count, 1, WIDE), F32),
                jax.ShapeDtypeStruct((count, 1, WIDE), F32),
                jax.ShapeDtypeStruct((count, HD, WIDE), F32),
            ],
            scratch_shapes=kv + tail,
            name="attend_first",
            **common,
        )(*args)
    return pl.pallas_call(
        second_kernel,
        in_specs=in_specs + held,
        out_specs=pl.BlockSpec((BLK, WIDE), lambda i: (i, 0)),
        out_shape=jax.ShapeDtypeStruct((count * BLK, WIDE), BF16),
        scratch_shapes=kv + [row, row, pltpu.VMEM((HD, WIDE), F32)] + tail,
        name="attend_second",
        **common,
    )(*args, *state)


def pack_kernel(keys, key_scale, values, value_scale, packed):
    for block in range(RANK_BLOCKS):
        rows = pl.ds(block * BLK, BLK)
        by_row = jnp.broadcast_to(key_scale[:, rows].astype(F32), (HD, BLK)).T
        packed[block, :, :HD] = (keys[rows].astype(F32) * by_row).astype(BF16)
        turned = values[rows].T.astype(F32) * value_scale[:, rows].astype(F32)
        packed[block, :, HD:] = turned.astype(BF16)


def pack(keys, key_scale, values, value_scale):
    vmem = pl.BlockSpec(memory_space=pltpu.VMEM)
    return pl.pallas_call(
        pack_kernel,
        in_specs=[vmem] * 4,
        out_specs=vmem,
        out_shape=jax.ShapeDtypeStruct((RANK_BLOCKS, BLK, 2 * HD), BF16),
        name="pack",
    )(keys, key_scale.T, values, value_scale.T)


def cut_kernel(info, weight, cut, stage, in_sems, out_sems):
    pieces, high, tile = cut.shape
    source = pl.ds(pl.multiple_of(info[2] * high, high), high)

    def copies(piece):
        first = pl.multiple_of(((1 - info[0]) * pieces + piece) * tile, tile)
        return (
            pltpu.make_async_copy(
                weight.at[source, pl.ds(first, tile)], stage.at[piece], in_sems.at[piece]
            ),
            pltpu.make_async_copy(stage.at[piece], cut.at[piece], out_sems.at[piece]),
        )

    loads = [copies(piece) for piece in range(pieces)]
    for load, _ in loads:
        load.start()
    for load, store in loads:
        load.wait()
        store.start()
    for _, store in loads:
        store.wait()


def cut_weights(info, weight):
    hbm = pl.BlockSpec(memory_space=pltpu.HBM)
    pieces = 4 * PARTS
    shape = (pieces, weight.shape[0] // 2, weight.shape[1] // 2 // pieces)
    return pl.pallas_call(
        cut_kernel,
        in_specs=[pl.BlockSpec(memory_space=pltpu.SMEM), hbm],
        out_specs=hbm,
        out_shape=jax.ShapeDtypeStruct(shape, BF16),
        scratch_shapes=[
            pltpu.VMEM(shape, BF16),
            pltpu.SemaphoreType.DMA((pieces,)),
            pltpu.SemaphoreType.DMA((pieces,)),
        ],
        compiler_params=pltpu.CompilerParams(vmem_limit_bytes=VMEM),
        cost_estimate=pl.CostEstimate(flops=0, bytes_accessed=16 << 20, transcendentals=0),
        name="cut",
    )(info, weight)


CORE_SWAP = [(i, i ^ 1) for i in range(2 * CHIPS)]


def along_x(block):
    got = [block]
    for shift in range(1, 4):
        pairs = [(4 * x + i, 4 * (x + shift) + i) for x in range(4 - shift) for i in range(4)]
        got.append(lax.ppermute(block, "ctx", pairs))
    return got


def with_core(got):
    mine = jnp.concatenate(got, axis=0)
    return mine, lax.ppermute(mine, "ctx", CORE_SWAP)


def across_y():
    pairs = []
    for x in range(4):
        for y in range(4):
            for core in range(2):
                for z in range(4):
                    far = (y + (1 if core == 0 else 3)) % 4
                    start = ((x * 2 + y // 2) * 2 + core) * HEADS + (y % 2) * 4 + z
                    end = ((x * 2 + far // 2) * 2 + core) * HEADS + (far % 2) * 4 + z
                    pairs.append((start, end))
    return pairs


def own_kernel(info, *refs):
    chunks = len(CHUNKS)
    own = refs[:chunks]
    weight, out, left, held, sems = refs[chunks:]
    tile = held.shape[2]

    def copies(shift):
        target = lax.rem(info[1] + shift, 4)
        mine = pl.ds(pl.multiple_of((info[0] * 4 + target) * tile, tile), tile)
        yield pltpu.make_async_copy(weight.at[:, mine], held.at[shift], sems.at[shift])

    for shift in range(4):
        for copy in copies(shift):
            copy.start()
    for at, (first, count) in enumerate(CHUNKS):
        left[pl.ds(first * BLK, count * BLK), :] = own[at][...]
    for shift in range(4):
        for copy in copies(shift):
            copy.wait()
        for at in range(RANK_BLOCKS):
            rows = pl.ds(at * BLK, BLK)
            value = jnp.dot(left[rows], held[shift], preferred_element_type=F32)
            width = out.shape[3]
            for part in range(PARTS):
                half = value[:, part * width : (part + 1) * width]
                out[part, shift, rows] = half.astype(BF16)


def project_own(info, own, weight):
    tile = weight.shape[1] // HEADS
    rows = RANK_BLOCKS * BLK
    vmem = pl.BlockSpec(memory_space=pltpu.VMEM)
    return pl.pallas_call(
        own_kernel,
        in_specs=[pl.BlockSpec(memory_space=pltpu.SMEM)]
        + [vmem] * len(CHUNKS)
        + [pl.BlockSpec(memory_space=pltpu.HBM)],
        out_specs=vmem,
        out_shape=jax.ShapeDtypeStruct((PARTS, 4, rows, tile // PARTS), BF16),
        scratch_shapes=[
            pltpu.VMEM((rows, WIDE), BF16),
            pltpu.VMEM((4, weight.shape[0], tile), BF16),
            pltpu.SemaphoreType.DMA((4,)),
        ],
        compiler_params=pltpu.CompilerParams(vmem_limit_bytes=VMEM),
        cost_estimate=pl.CostEstimate(
            flops=2 * rows * WIDE * 4 * tile,
            bytes_accessed=WIDE * 4 * tile * 2 + rows * WIDE * 10,
            transcendentals=0,
        ),
        name="project_own",
    )(info, *own, weight)


ORDER = (2, 1, 3, 0)


def partner_kernel(part, info, *refs):
    chunks = len(CHUNKS)
    partner = refs[:chunks]
    base, near, far = refs[chunks : chunks + 3]
    outs = refs[chunks + 3 :][:4]
    left, held, begun, sems = refs[-4:]
    keep = near.shape[1]

    def copies(at):
        shift = ORDER[at]
        piece = lax.rem(info[1] + shift, 4) * PARTS + part
        for which, source in ((0, near), (1, far)):
            half = lax.rem(info[2] + which, 2)
            rows = pl.ds(pl.multiple_of(half * keep, keep), keep)
            yield pltpu.make_async_copy(
                source.at[piece], held.at[shift, rows], sems.at[shift, which]
            )
        yield pltpu.make_async_copy(base.at[part, shift], begun.at[shift], sems.at[shift, 2])

    for at in range(2):
        for copy in copies(at):
            copy.start()
    for at, (first, count) in enumerate(CHUNKS):
        left[pl.ds(first * BLK, count * BLK), :] = partner[at][...]
    for at, shift in enumerate(ORDER):
        for copy in copies(at):
            copy.wait()
        if at + 2 < len(ORDER):
            for copy in copies(at + 2):
                copy.start()
        for block in range(RANK_BLOCKS):
            rows = pl.ds(block * BLK, BLK)
            value = jnp.dot(left[rows], held[shift], preferred_element_type=F32)
            outs[shift][rows] = (value + begun[shift, rows].astype(F32)).astype(BF16)


def project_partner(info, partner, base, near, far, part):
    _, _, rows, tile = base.shape
    vmem = pl.BlockSpec(memory_space=pltpu.VMEM)
    hbm = pl.BlockSpec(memory_space=pltpu.HBM)
    return pl.pallas_call(
        functools.partial(partner_kernel, part),
        in_specs=[pl.BlockSpec(memory_space=pltpu.SMEM)] + [vmem] * len(CHUNKS) + [hbm] * 3,
        out_specs=[vmem] * 4,
        out_shape=[jax.ShapeDtypeStruct((rows, tile), BF16)] * 4,
        scratch_shapes=[
            pltpu.VMEM((rows, WIDE), BF16),
            pltpu.VMEM((4, WIDE, tile), BF16),
            pltpu.VMEM((4, rows, tile), BF16),
            pltpu.SemaphoreType.DMA((4, 3)),
        ],
        compiler_params=pltpu.CompilerParams(vmem_limit_bytes=20 << 20),
        cost_estimate=pl.CostEstimate(
            flops=2 * rows * WIDE * 4 * tile,
            bytes_accessed=WIDE * 4 * tile * 2 + rows * WIDE * 8,
            transcendentals=0,
        ),
        name="project_partner",
    )(info, *partner, base, near, far)


def ring(block, step):
    return lax.ppermute(block, "head", [(i, i // 4 * 4 + (i + step) % 4) for i in range(HEADS)])


def sum_over_z(sums, clockwise):
    own, ahead, across, behind = sums
    step = 1 if clockwise else -1
    first, second = (ahead, behind) if clockwise else (behind, ahead)
    passed = ring(across, step)
    direct = ring(second, -step)
    joined = ring((first.astype(F32) + passed.astype(F32)).astype(BF16), step)
    return own.astype(F32) + direct.astype(F32) + joined.astype(F32)


def local(
    queries, query_scale, keys, key_scale, values, value_scale, block_mask, out_weight, out_scale
):
    rank = lax.axis_index("ctx").astype(jnp.int32)
    head = lax.axis_index("head").astype(jnp.int32)
    place = jnp.stack([rank // 2, rank % 2, rank * RANK_BLOCKS])
    info = jnp.stack([head // 4, head % 4, rank % 2])
    packed = pack(keys, key_scale, values, value_scale)
    cut = cut_weights(info, out_weight)
    beside = lax.ppermute(packed, "ctx", [(i, i ^ 2) for i in range(2 * CHIPS)])
    along = along_x(packed)
    cut, beside = lax.optimization_barrier((cut, beside))
    near = lax.ppermute(cut, ("ctx", "head"), across_y())
    along, beside = lax.optimization_barrier((along, beside))
    first_kv = with_core(along)
    state = attend(
        place, block_mask, queries, query_scale, *first_kv, (0, RANK_BLOCKS), None
    )
    later, state = lax.optimization_barrier((along_x(beside), state))
    second_kv = with_core(later)
    own, partner = [], []
    for at, chunk in enumerate(CHUNKS):
        rows = attend(place, block_mask, queries, query_scale, *second_kv, chunk, state)
        rows, state = lax.optimization_barrier((rows, state))
        own.append(rows)
        partner.append(lax.ppermute(rows, "head", [(i, i ^ 4) for i in range(HEADS)]))
        if at == 1:
            partner[0], state = lax.optimization_barrier((partner[0], state))
    own, partner[1], near = lax.optimization_barrier((own, partner[1], near))
    base = project_own(info, own, out_weight)
    far = lax.ppermute(near, "ctx", CORE_SWAP)
    parts = []
    for part in range(PARTS):
        sums = project_partner(info, partner, base, near, far, part)
        parts.append(sum_over_z(sums, part % 2 == 0))
    return (jnp.concatenate(parts, axis=1) * out_scale[None, :]).astype(BF16)


def solution(mesh):
    return jax.shard_map(
        local,
        mesh=mesh,
        in_specs=(
            P("ctx", "head"),
            P("ctx", "head"),
            P("ctx", "head"),
            P("ctx", "head"),
            P("ctx", "head"),
            P("ctx", "head"),
            P(),
            P("head", None),
            P("head"),
        ),
        out_specs=P("ctx", "head"),
        check_vma=False,
    )
```
